32 devices in a mesh: tm: 8 (over z, y), port: 4 (over x, core).
Axes of the slice: x: 2, y: 2, z: 4, core: 2. Of those that a mesh axis runs over, the one named last changes fastest.
Arguments:
- voltages: float32 [256, 131072], P('port', 'tm'), may hold values from -6 to 6
- currents: float32 [256, 131072], P('port', 'tm'), may hold values from -0.12 to 0.12
- impedance: float32 [256], P('port'), may hold values from 25 to 100
- freq_index: int32 [2048], replicated, may hold values from 1 to 65535
- window_start: int32 [256], P('port'), may hold values from 0 to 65535
- pairing: int32 [256], P('port'), may hold values from 0 to 255
Outputs:
- scattering: float32 [2, 256, 2048], P(None, 'port', 'tm')
The draws below stay inside these ranges and needn't reach their ends.
All inputs are finite; a program needn't handle non-finite values.
Results may differ from the reference program's by a relative error of at most 0.011.
Values sent between devices are 32-bit elements; how exact they have to be, the bound alone decides.
A program may use at most 128 MiB of HBM per device.

```python
import math
import jax
import jax.numpy as jnp
from jax import lax

P_SIZE = 256
F = 2048
NT = 131072


def plant(entries, rng, least, top_value):
    spot = [jax.random.randint(jax.random.fold_in(rng, axis), (), 0, length) for axis, length in enumerate(entries.shape)]
    longest = entries.shape.index(max(entries.shape))
    neighbour = spot[:longest] + [(spot[longest] + 1) % entries.shape[longest]] + spot[longest + 1:]
    return entries.at[tuple(spot)].set(least).at[tuple(neighbour)].set(top_value)


def block_levels(own_key, shape, shards, low, largest):
    loudness, own = 1.0, jax.random.fold_in(own_key, 6)
    for axis_at, parts in shards:
        steps = jnp.exp(jax.random.uniform(jax.random.fold_in(own, axis_at), (parts,), jnp.float32, low / len(shards), largest / len(shards)))
        loudness = loudness * jnp.repeat(steps, shape[axis_at] // parts).reshape([-1 if axis == axis_at else 1 for axis in range(len(shape))])
    return loudness


def gaussian(rng, shape, scale, limit, pieces=(), kind=jnp.bfloat16):
    gain = block_levels(rng, shape, pieces, -0.22, 0.18) if pieces else 1.0
    drawn = jax.random.normal(rng, shape, jnp.float32) * scale * gain
    return jnp.minimum(jnp.maximum(drawn, -limit), limit).astype(kind)


def setup_inputs(seed: int = 0) -> dict:
    arg_keys = jax.random.split(jax.random.key(seed), 7)
    voltages = gaussian(arg_keys[0], (P_SIZE, NT), 1.0, 6.0, ((0, 4), (1, 8)), jnp.float32)
    currents = gaussian(arg_keys[1], (P_SIZE, NT), 0.02, 0.12, ((0, 4), (1, 8)), jnp.float32)
    impedance = jnp.clip(jnp.exp(math.log(100.0) - 1.3862944 * jax.random.uniform(arg_keys[2], (P_SIZE,), jnp.float32) ** block_levels(arg_keys[2], (P_SIZE,), ((0, 4),), -0.2, 0.2)), 25.0, 100.0)
    freq_index = plant(jax.random.randint(arg_keys[3], (F,), 1, NT // 2), jax.random.fold_in(arg_keys[3], 1), 1, (NT // 2) - 1).astype(jnp.int32)
    window_start = plant(jax.random.randint(arg_keys[4], (P_SIZE,), 0, NT // 2), jax.random.fold_in(arg_keys[4], 1), 0, (NT // 2) - 1).astype(jnp.int32)
    pairing = plant(jax.random.randint(arg_keys[5], (P_SIZE,), 0, P_SIZE), jax.random.fold_in(arg_keys[5], 1), 0, P_SIZE - 1).astype(jnp.int32)
    return {"voltages": voltages, "currents": currents, "impedance": impedance, "freq_index": freq_index, "window_start": window_start, "pairing": pairing}


def twiddles(freq_index, times, total):
    high = freq_index // 512
    low = freq_index % 512
    stride = times * 512 % total
    phase = (stride[:, None] * high[None, :] % total + times[:, None] * low[None, :]) % total
    angle = phase.astype(jnp.float32) * (2.0 * math.pi / total)
    return jnp.concatenate([jnp.cos(angle), -jnp.sin(angle)], axis=1).astype(jnp.bfloat16)

def waves(spec_v, spec_c, impedance, width):
    zcol = impedance[:, None]
    root = 2.0 * jnp.sqrt(zcol)
    v_re, v_im = (spec_v[:, :width], spec_v[:, width:])
    c_re, c_im = (spec_c[:, :width], spec_c[:, width:])
    a_re = (v_re + zcol * c_re) / root
    a_im = (v_im + zcol * c_im) / root
    b_re = (v_re - zcol * c_re) / root
    b_im = (v_im - zcol * c_im) / root
    return (a_re, a_im, b_re, b_im)

def reference(voltages, currents, impedance, freq_index, window_start, pairing):
    ports, total = voltages.shape
    width = freq_index.shape[0]
    block = math.gcd(total, 8192)
    times_all = jnp.arange(total, dtype=jnp.int32)
    gate = times_all[None, :] >= window_start[:, None]
    gated_v = jnp.where(gate, voltages, 0.0).astype(jnp.bfloat16)
    gated_c = jnp.where(gate, currents, 0.0).astype(jnp.bfloat16)

    def accumulate(carry, index):
        start = index * block
        times = start + jnp.arange(block, dtype=jnp.int32)
        table = twiddles(freq_index, times, total)
        part_v = lax.dynamic_slice_in_dim(gated_v, start, block, 1)
        part_c = lax.dynamic_slice_in_dim(gated_c, start, block, 1)
        return ((carry[0] + jnp.dot(part_v, table, preferred_element_type=jnp.float32), carry[1] + jnp.dot(part_c, table, preferred_element_type=jnp.float32)), None)
    empty = jnp.zeros((ports, 2 * width), jnp.float32)
    (sum_v, sum_c), _ = lax.scan(accumulate, (empty, empty), jnp.arange(total // block, dtype=jnp.int32))
    scale = 1.0 / math.sqrt(total)
    a_re, a_im, b_re, b_im = waves(sum_v * scale, sum_c * scale, impedance, width)
    power = a_re * a_re + a_im * a_im
    mean_power = lax.optimization_barrier(jnp.sum(power, axis=1)) / width + 1e-06
    q_re = jnp.take(a_re, pairing, axis=0)
    q_im = jnp.take(a_im, pairing, axis=0)
    q_power = jnp.take(power, pairing, axis=0)
    q_mean = jnp.take(mean_power, pairing, axis=0)
    denom = jnp.maximum(q_power, 0.1 * q_mean[:, None])
    s_re = (b_re * q_re + b_im * q_im) / denom
    s_im = (b_im * q_re - b_re * q_im) / denom
    return jnp.stack([s_re, s_im], axis=0)
```

```python
import functools
import math

import jax
import jax.numpy as jnp
from jax import lax
from jax.experimental import pallas as pl
from jax.experimental.pallas import tpu as pltpu
from jax.sharding import PartitionSpec as P

BASE = 32
F32 = jnp.float32


def kernel(
    sizes,
    v_hbm, c_hbm, cos_ref, sin_ref, z_ref, start_ref, pair_ref,
    out_ref,
    xv, xc, xe, xo, tab_c, tab_s, away, own, y_recv, z_recv, gath, pbuf, mbuf, mcol, qa, qm,
    load_sem, y_send, y_got, z_send, z_got, g_send, g_got, p_send, p_got, m_send, m_got,
):
    n_tm, n_in, n_port, ports, half, blocks, lines, groups, width = sizes
    n_out = n_tm // n_in
    rows = 2 * ports
    me = lax.axis_index("tm")
    port = lax.axis_index("port")
    outer, inner = me // n_in, lax.rem(me, n_in)
    span = 2 * half

    def load(block, which):
        source, target = ((v_hbm, xv), (c_hbm, xc))[which]
        return pltpu.make_async_copy(
            source.at[:, pl.ds(pl.multiple_of(block * span, span), span)],
            target.at[:, pl.ds(pl.multiple_of(block * span, span), span)],
            load_sem.at[which, block],
        )

    for block in range(blocks):
        for which in range(2):
            load(block, which).start()

    barrier = pltpu.get_barrier_semaphore()
    for step in range(1, n_tm):
        pl.semaphore_signal(barrier, inc=1, device_id={"tm": lax.rem(me + step, n_tm)})
    for step in range(1, n_port):
        pl.semaphore_signal(barrier, inc=1, device_id={"port": lax.rem(port + step, n_port)})

    flip = (
        lax.broadcasted_iota(jnp.int32, (128, 128), 0)
        + lax.broadcasted_iota(jnp.int32, (128, 128), 1)
        == 127
    ).astype(F32).astype(jnp.bfloat16)
    tiles = half // 128
    lane = lax.broadcasted_iota(jnp.int32, (ports, 128), 1)
    starts = jnp.broadcast_to(start_ref[...], (ports, 128)) - me * (blocks * span) - lane

    def fold(block, carry):
        for which in range(2):
            load(block, which).wait()
            ref = (xv, xc)[which]

            def piece(tile):
                at = pl.multiple_of(block * span + tile * 128, 128)
                entries = jnp.where(starts <= at, ref[:, pl.ds(at, 128)], 0.0)
                return entries.astype(jnp.bfloat16)

            at_row = pl.multiple_of(block * rows + which * ports, ports)
            for tile in range(tiles):
                later = piece(tiles + tile).astype(F32)
                earlier = jnp.dot(piece(tiles - 1 - tile), flip, preferred_element_type=F32)
                xe[pl.ds(at_row, ports), tile * 128:(tile + 1) * 128] = (later + earlier).astype(jnp.bfloat16)
                xo[pl.ds(at_row, ports), tile * 128:(tile + 1) * 128] = (later - earlier).astype(jnp.bfloat16)
        return carry

    lax.fori_loop(0, blocks, fold, 0)
    pl.semaphore_wait(barrier, n_tm - 1 + n_port - 1)

    def spectra(owner, store):
        at = pl.ds(pl.multiple_of(owner * lines, lines), lines)
        bc, bs = cos_ref[0:BASE, at], sin_ref[0:BASE, at]
        for g in range(groups):
            tc, ts = cos_ref[BASE + g:BASE + g + 1, at], sin_ref[BASE + g:BASE + g + 1, at]
            tab_c[g * BASE:(g + 1) * BASE, :] = (tc * bc - ts * bs).astype(jnp.bfloat16)
            tab_s[g * BASE:(g + 1) * BASE, :] = (ts * bc + tc * bs).astype(jnp.bfloat16)
        even = jnp.dot(xe[...], tab_c[...], preferred_element_type=F32)
        odd = jnp.dot(xo[...], tab_s[...], preferred_element_type=F32)
        re = jnp.zeros((rows, lines), F32)
        im = jnp.zeros((rows, lines), F32)
        for block in range(blocks):
            k = BASE + groups + block
            pc, ps = cos_ref[k:k + 1, at], sin_ref[k:k + 1, at]
            e, o = even[block * rows:(block + 1) * rows], odd[block * rows:(block + 1) * rows]
            re = re + (pc * e - ps * o)
            im = im - (ps * e + pc * o)
        store[:, 0:lines] = re
        store[:, lines:2 * lines] = im

    def y_copy(k, r):
        return pltpu.make_async_remote_copy(
            src_ref=away.at[k, r], dst_ref=y_recv.at[k, r],
            send_sem=y_send.at[k, r], recv_sem=y_got.at[k, r],
            device_id={"tm": outer * n_in + lax.rem(inner + 1 + r, n_in)},
        )

    def z_copy(k):
        return pltpu.make_async_remote_copy(
            src_ref=own.at[k], dst_ref=z_recv.at[k],
            send_sem=z_send.at[k], recv_sem=z_got.at[k],
            device_id={"tm": lax.rem(outer + k + 1, n_out) * n_in + inner},
        )

    def collect(k):
        for r in range(n_in - 1):
            y_copy(k, r).wait_recv()
            own[k] = own[k] + y_recv[k, r]

    def stage(k, carry):
        target = lax.rem(outer + k + 1, n_out)
        for r in range(n_in - 1):
            spectra(target * n_in + lax.rem(inner + 1 + r, n_in), away.at[k, r])
            y_copy(k, r).start()
        spectra(target * n_in + inner, own.at[k])

        @pl.when(k >= 1)
        def _():
            collect(k - 1)
            z_copy(k - 1).start()

        return carry

    lax.fori_loop(0, n_out, stage, 0)
    collect(n_out - 1)
    total = own[n_out - 1]
    for k in range(n_out - 1):
        z_copy(k).wait_recv()
        total = total + z_recv[k]

    volts, amps = total[0:ports], total[ports:rows]
    zcol = z_ref[...]
    root = 2.0 * jnp.sqrt(zcol)
    a = (volts + zcol * amps) / root
    b = (volts - zcol * amps) / root
    mine = pl.ds(pl.multiple_of(port * ports, ports), ports)
    gath[mine, :] = a

    def g_copy(step):
        return pltpu.make_async_remote_copy(
            src_ref=gath.at[mine, :], dst_ref=gath.at[mine, :],
            send_sem=g_send.at[step - 1], recv_sem=g_got.at[step - 1],
            device_id={"port": lax.rem(port + step, n_port)},
        )

    def p_copy(step):
        return pltpu.make_async_remote_copy(
            src_ref=pbuf.at[0], dst_ref=pbuf.at[step],
            send_sem=p_send.at[step - 1], recv_sem=p_got.at[step - 1],
            device_id={"tm": lax.rem(me + step, n_tm)},
        )

    def m_copy(step):
        return pltpu.make_async_remote_copy(
            src_ref=mbuf.at[port], dst_ref=mbuf.at[port],
            send_sem=m_send.at[step - 1], recv_sem=m_got.at[step - 1],
            device_id={"port": lax.rem(port + step, n_port)},
        )

    a_re, a_im = a[:, 0:lines], a[:, lines:2 * lines]
    power = jnp.sum(a_re * a_re + a_im * a_im, axis=1, keepdims=True)
    diagonal = lane == lax.broadcasted_iota(jnp.int32, (ports, 128), 0)
    packed = jnp.sum(jnp.where(diagonal, power, 0.0), axis=0, keepdims=True)
    pbuf[0] = jnp.broadcast_to(packed, (8, 128))
    for step in range(1, n_tm):
        p_copy(step).start()
    for step in range(1, n_port):
        g_copy(step).start()
    powers = pbuf[0]
    for step in range(1, n_tm):
        p_copy(step).wait_recv()
        powers = powers + pbuf[step]
    mbuf[port] = powers / width + 1e-06
    for step in range(1, n_port):
        m_copy(step).start()
    for step in range(1, n_port):
        m_copy(step).wait_recv()
    for index in range(n_port):
        spread = jnp.broadcast_to(mbuf[index][0:1, :], (ports, 128))
        column = jnp.sum(jnp.where(diagonal, spread, 0.0), axis=1, keepdims=True)
        mcol[index * ports:(index + 1) * ports, :] = jnp.broadcast_to(column, (ports, 128))
    for step in range(1, n_port):
        g_copy(step).wait_recv()
    for p in range(ports):
        q = pair_ref[p]
        qa[p:p + 1, :] = gath[pl.ds(q, 1), :]
        qm[p:p + 1, :] = mcol[pl.ds(q, 1), :]
    q_re, q_im = qa[:, 0:lines], qa[:, lines:2 * lines]
    denom = jnp.maximum(q_re * q_re + q_im * q_im, 0.1 * qm[:, 0:1])
    b_re, b_im = b[:, 0:lines], b[:, lines:2 * lines]
    out_ref[0] = (b_re * q_re + b_im * q_im) / denom
    out_ref[1] = (b_im * q_re - b_re * q_im) / denom

    for k in range(n_out):
        for r in range(n_in - 1):
            y_copy(k, r).wait_send()
    for k in range(n_out - 1):
        z_copy(k).wait_send()
    for step in range(1, n_tm):
        p_copy(step).wait_send()
    for step in range(1, n_port):
        g_copy(step).wait_send()
        m_copy(step).wait_send()


def body(n_tm, n_port, voltages, currents, impedance, freq_index, window_start, pairing):
    ports, local_times = voltages.shape
    width = freq_index.shape[0]
    total = local_times * n_tm
    assert total & (total - 1) == 0 and ports <= 128
    half = math.gcd(local_times // 2, 1024)
    blocks = local_times // (2 * half)
    groups = half // BASE
    lines = width // n_tm
    n_in = 2 if n_tm < 16 else 4
    n_out = n_tm // n_in
    rows = 2 * ports
    first = lax.axis_index("tm") * local_times
    odd_steps = 2 * jnp.arange(BASE, dtype=jnp.int32) + 1
    turns = 2 * BASE * jnp.arange(groups, dtype=jnp.int32)
    centres = 2 * first + 4 * half * jnp.arange(blocks, dtype=jnp.int32) + 2 * half - 1
    steps = jnp.concatenate([odd_steps, turns, centres])
    scale = jnp.where(jnp.arange(steps.shape[0]) < BASE + groups, 1.0, 1.0 / math.sqrt(total)).astype(F32)
    phase = (steps[:, None] * freq_index[None, :]) & (2 * total - 1)
    angle = phase.astype(F32) * (math.pi / total)
    cosines = jnp.cos(angle) * scale[:, None]
    sines = jnp.sin(angle) * scale[:, None]

    sizes = (n_tm, n_in, n_port, ports, half, blocks, lines, groups, width)
    vmem = pl.BlockSpec(memory_space=pltpu.VMEM)
    dma = pltpu.SemaphoreType.DMA
    return pl.pallas_call(
        functools.partial(kernel, sizes),
        out_shape=jax.ShapeDtypeStruct((2, ports, lines), F32),
        in_specs=[
            pl.BlockSpec(memory_space=pl.ANY), pl.BlockSpec(memory_space=pl.ANY),
            vmem, vmem, vmem, vmem, pl.BlockSpec(memory_space=pltpu.SMEM),
        ],
        out_specs=vmem,
        scratch_shapes=[
            pltpu.VMEM((ports, local_times), F32),
            pltpu.VMEM((ports, local_times), F32),
            pltpu.VMEM((blocks * rows, half), jnp.bfloat16),
            pltpu.VMEM((blocks * rows, half), jnp.bfloat16),
            pltpu.VMEM((half, lines), jnp.bfloat16),
            pltpu.VMEM((half, lines), jnp.bfloat16),
            pltpu.VMEM((n_out, n_in - 1, rows, 2 * lines), F32),
            pltpu.VMEM((n_out, rows, 2 * lines), F32),
            pltpu.VMEM((n_out, n_in - 1, rows, 2 * lines), F32),
            pltpu.VMEM((n_out - 1, rows, 2 * lines), F32),
            pltpu.VMEM((n_port * ports, 2 * lines), F32),
            pltpu.VMEM((n_tm, 8, 128), F32),
            pltpu.VMEM((n_port, 8, 128), F32),
            pltpu.VMEM((n_port * ports, 128), F32),
            pltpu.VMEM((ports, 2 * lines), F32),
            pltpu.VMEM((ports, 128), F32),
            dma((2, blocks)),
            dma((n_out, n_in - 1)), dma((n_out, n_in - 1)),
            dma((n_out - 1,)), dma((n_out - 1,)),
            dma((n_port - 1,)), dma((n_port - 1,)),
            dma((n_tm - 1,)), dma((n_tm - 1,)),
            dma((n_port - 1,)), dma((n_port - 1,)),
        ],
        compiler_params=pltpu.CompilerParams(
            collective_id=0, has_side_effects=True, vmem_limit_bytes=56 * 2**20
        ),
        name="spectra",
    )(voltages, currents, cosines, sines, impedance[:, None], window_start[:, None], pairing)


def solution(mesh):
    placed = (P("port", "tm"), P("port", "tm"), P("port"), P(), P("port"), P("port"))
    return jax.shard_map(
        functools.partial(body, mesh.shape["tm"], mesh.shape["port"]),
        mesh=mesh, in_specs=placed, out_specs=P(None, "port", "tm"), check_vma=False,
    )
```

```python
import functools
import math

import jax
import jax.numpy as jnp
from jax import lax
from jax.experimental import pallas as pl
from jax.experimental.pallas import tpu as pltpu
from jax.sharding import PartitionSpec as P

BASE = 32
F32 = jnp.float32


def kernel(
    sizes,
    v_hbm, c_hbm, freq_ref, z_ref, start_ref, pair_ref,
    out_ref,
    cos_ref, sin_ref,
    xv, xc, xe, xo, tab_c, tab_s, away, own, y_recv, z_recv, gath, pbuf, mbuf, mcol, qa, qm,
    load_sem, y_send, y_got, z_send, z_got, g_send, g_got, p_send, p_got, m_send, m_got,
):
    n_tm, n_in, n_port, ports, half, blocks, lines, groups, width, subs = sizes
    sub = lines // subs
    n_out = n_tm // n_in
    rows = 2 * ports
    me = lax.axis_index("tm")
    port = lax.axis_index("port")
    outer, inner = me // n_in, lax.rem(me, n_in)
    span = 2 * half

    def load(block, which):
        source, target = ((v_hbm, xv), (c_hbm, xc))[which]
        return pltpu.make_async_copy(
            source.at[:, pl.ds(pl.multiple_of(block * span, span), span)],
            target.at[:, pl.ds(pl.multiple_of(block * span, span), span)],
            load_sem.at[which, block],
        )

    for block in range(blocks):
        for which in range(2):
            load(block, which).start()

    barrier = pltpu.get_barrier_semaphore()
    for step in range(1, n_tm):
        pl.semaphore_signal(barrier, inc=1, device_id={"tm": lax.rem(me + step, n_tm)})
    for step in range(1, n_port):
        pl.semaphore_signal(barrier, inc=1, device_id={"port": lax.rem(port + step, n_port)})

    flip = (
        lax.broadcasted_iota(jnp.int32, (128, 128), 0)
        + lax.broadcasted_iota(jnp.int32, (128, 128), 1)
        == 127
    ).astype(F32).astype(jnp.bfloat16)
    tiles = half // 128
    lane = lax.broadcasted_iota(jnp.int32, (ports, 128), 1)
    square = lax.broadcasted_iota(jnp.int32, (ports, ports), 0) == lax.broadcasted_iota(
        jnp.int32, (ports, ports), 1
    )

    def column_of(row):
        return jnp.sum(jnp.where(square, row, 0.0), axis=1, keepdims=True)

    zcol = column_of(z_ref[...])
    start_column = column_of(start_ref[...].astype(F32)).astype(jnp.int32)
    starts = jnp.broadcast_to(start_column, (ports, 128)) - me * (blocks * span) - lane

    whole = n_tm * blocks * span
    quarter_bits = (whole // 2).bit_length() - 1
    freq = freq_ref[...]
    count = lax.broadcasted_iota(jnp.int32, (8, 1), 0)
    for at in range(0, BASE + groups + blocks, 8):
        scale = 1.0
        if at < BASE:
            steps = 2 * (count + at) + 1
        elif at < BASE + groups:
            steps = 2 * BASE * (count + (at - BASE))
        else:
            scale = 1.0 / math.sqrt(whole)
            steps = me * (2 * blocks * span) + 4 * half * (count + (at - BASE - groups)) + (2 * half - 1)
        phase = (steps * freq) & (2 * whole - 1)
        quarter = (phase + whole // 4) >> quarter_bits
        x = (phase - (quarter << quarter_bits)).astype(F32) * (math.pi / whole)
        xx = x * x
        s = x * (1.0 + xx * (-1 / 6 + xx * (1 / 120 + xx * (-1 / 5040 + xx * (1 / 362880)))))
        c = 1.0 + xx * (-1 / 2 + xx * (1 / 24 + xx * (-1 / 720 + xx * (1 / 40320))))
        swap = (quarter & 1) == 1
        cosine, sine = jnp.where(swap, s, c), jnp.where(swap, c, s)
        cos_ref[at:at + 8, :] = jnp.where(((quarter + 1) & 2) == 2, -cosine, cosine) * scale
        sin_ref[at:at + 8, :] = jnp.where((quarter & 2) == 2, -sine, sine) * scale

    def fold(block, carry):
        for which in range(2):
            load(block, which).wait()
            ref = (xv, xc)[which]

            def piece(tile):
                at = pl.multiple_of(block * span + tile * 128, 128)
                entries = jnp.where(starts <= at, ref[:, pl.ds(at, 128)], 0.0)
                return entries.astype(jnp.bfloat16)

            at_row = pl.multiple_of(block * rows + which * ports, ports)
            for tile in range(tiles):
                later = piece(tiles + tile).astype(F32)
                earlier = jnp.dot(piece(tiles - 1 - tile), flip, preferred_element_type=F32)
                xe[pl.ds(at_row, ports), tile * 128:(tile + 1) * 128] = (later + earlier).astype(jnp.bfloat16)
                xo[pl.ds(at_row, ports), tile * 128:(tile + 1) * 128] = (later - earlier).astype(jnp.bfloat16)
        return carry

    lax.fori_loop(0, blocks, fold, 0)
    pl.semaphore_wait(barrier, n_tm - 1 + n_port - 1)

    def spectra(owner, store):
        at = pl.ds(pl.multiple_of(owner * lines, lines), lines)
        bc, bs = cos_ref[0:BASE, at], sin_ref[0:BASE, at]
        for g in range(groups):
            tc, ts = cos_ref[BASE + g:BASE + g + 1, at], sin_ref[BASE + g:BASE + g + 1, at]
            tab_c[g * BASE:(g + 1) * BASE, :] = (tc * bc - ts * bs).astype(jnp.bfloat16)
            tab_s[g * BASE:(g + 1) * BASE, :] = (ts * bc + tc * bs).astype(jnp.bfloat16)
        even = jnp.dot(xe[...], tab_c[...], preferred_element_type=F32)
        odd = jnp.dot(xo[...], tab_s[...], preferred_element_type=F32)
        re = jnp.zeros((rows, lines), F32)
        im = jnp.zeros((rows, lines), F32)
        for block in range(blocks):
            k = BASE + groups + block
            pc, ps = cos_ref[k:k + 1, at], sin_ref[k:k + 1, at]
            e, o = even[block * rows:(block + 1) * rows], odd[block * rows:(block + 1) * rows]
            re = re + (pc * e - ps * o)
            im = im - (ps * e + pc * o)
        for h in range(subs):
            store[h, :, 0:sub] = re[:, h * sub:(h + 1) * sub]
            store[h, :, sub:2 * sub] = im[:, h * sub:(h + 1) * sub]

    def destination(k):
        code, step, place, bit = 0, n_out - 1 - k, outer, 1
        for _ in range((n_out - 1).bit_length()):
            one, two = lax.rem(step, 2), lax.rem(place, 2)
            code = code + bit * (one + two - 2 * one * two)
            step, place, bit = step // 2, place // 2, 2 * bit
        return code

    def y_copy(k, r, h):
        return pltpu.make_async_remote_copy(
            src_ref=away.at[k, r, h], dst_ref=y_recv.at[k, r, h],
            send_sem=y_send.at[k, r, h], recv_sem=y_got.at[k, r, h],
            device_id={"tm": outer * n_in + lax.rem(inner + 1 + r, n_in)},
        )

    def z_copy(k, d, h, side):
        step = 1 - 2 * side
        return pltpu.make_async_remote_copy(
            src_ref=own.at[k, h], dst_ref=z_recv.at[side, d, h],
            send_sem=z_send.at[k, h], recv_sem=z_got.at[side, d, h],
            device_id={"tm": (outer + step) * n_in + inner},
        )

    def add_side(k, d, h, side):
        @pl.when(outer > 0 if side == 0 else outer < n_out - 1)
        def _():
            z_copy(k, d, h, side).wait_recv()
            own[k, h] = own[k, h] + z_recv[side, d, h]

    def collect(k, h):
        for r in range(n_in - 1):
            y_copy(k, r, h).wait_recv()
            own[k, h] = own[k, h] + y_recv[k, r, h]

    def service(k):
        d = destination(k)
        for h in range(subs):
            collect(k, h)

            @pl.when(d > outer)
            def _():
                add_side(k, d, h, 0)
                z_copy(k, d, h, 0).start()

            @pl.when(d < outer)
            def _():
                add_side(k, d, h, 1)
                z_copy(k, d, h, 1).start()

    def stage(k, carry):
        target = destination(k)
        for r in range(n_in - 1):
            spectra(target * n_in + lax.rem(inner + 1 + r, n_in), away.at[k, r])
            for h in range(subs):
                y_copy(k, r, h).start()
        spectra(target * n_in + inner, own.at[k])

        @pl.when(k >= 1)
        def _():
            service(k - 1)

        return carry

    lax.fori_loop(0, n_out, stage, 0)

    mine = pl.ds(pl.multiple_of(port * ports, ports), ports)

    def g_copy(step, h):
        return pltpu.make_async_remote_copy(
            src_ref=gath.at[h, mine, :], dst_ref=gath.at[h, mine, :],
            send_sem=g_send.at[step - 1, h], recv_sem=g_got.at[step - 1, h],
            device_id={"port": lax.rem(port + step, n_port)},
        )

    root = 2.0 * jnp.sqrt(zcol)
    power = jnp.zeros((ports, 1), F32)
    for h in range(subs):
        collect(n_out - 1, h)
        add_side(n_out - 1, outer, h, 0)
        add_side(n_out - 1, outer, h, 1)
        volts, amps = own[n_out - 1, h, 0:ports], own[n_out - 1, h, ports:2 * ports]
        a = (volts + zcol * amps) / root
        gath[h, mine, :] = a
        for step in range(1, n_port):
            g_copy(step, h).start()
        power = power + jnp.sum(a * a, axis=1, keepdims=True)

    def p_copy(step):
        return pltpu.make_async_remote_copy(
            src_ref=pbuf.at[0], dst_ref=pbuf.at[step],
            send_sem=p_send.at[step - 1], recv_sem=p_got.at[step - 1],
            device_id={"tm": lax.rem(me + step, n_tm)},
        )

    def m_copy(step):
        return pltpu.make_async_remote_copy(
            src_ref=mbuf.at[port], dst_ref=mbuf.at[port],
            send_sem=m_send.at[step - 1], recv_sem=m_got.at[step - 1],
            device_id={"port": lax.rem(port + step, n_port)},
        )

    diagonal = lane == lax.broadcasted_iota(jnp.int32, (ports, 128), 0)
    packed = jnp.sum(jnp.where(diagonal, power, 0.0), axis=0, keepdims=True)
    pbuf[0] = jnp.broadcast_to(packed, (8, 128))
    for step in range(1, n_tm):
        p_copy(step).start()
    powers = pbuf[0]
    for step in range(1, n_tm):
        p_copy(step).wait_recv()
        powers = powers + pbuf[step]
    mbuf[port] = powers / width + 1e-06
    for step in range(1, n_port):
        m_copy(step).start()
    for step in range(1, n_port):
        m_copy(step).wait_recv()
    for index in range(n_port):
        spread = jnp.broadcast_to(mbuf[index][0:1, :], (ports, 128))
        column = jnp.sum(jnp.where(diagonal, spread, 0.0), axis=1, keepdims=True)
        mcol[index * ports:(index + 1) * ports, :] = jnp.broadcast_to(column, (ports, 128))
    for h in range(subs):
        for step in range(1, n_port):
            g_copy(step, h).wait_recv()
    for p in range(ports):
        q = pair_ref[p]
        for h in range(subs):
            qa[h, p:p + 1, :] = gath[h, pl.ds(q, 1), :]
        qm[p:p + 1, :] = mcol[pl.ds(q, 1), :]
    least = 0.1 * qm[:, 0:1]
    for h in range(subs):
        volts, amps = own[n_out - 1, h, 0:ports], own[n_out - 1, h, ports:2 * ports]
        b = (volts - zcol * amps) / root
        b_re, b_im = b[:, 0:sub], b[:, sub:2 * sub]
        q_re, q_im = qa[h, :, 0:sub], qa[h, :, sub:2 * sub]
        denom = jnp.maximum(q_re * q_re + q_im * q_im, least)
        out_ref[0, :, h * sub:(h + 1) * sub] = (b_re * q_re + b_im * q_im) / denom
        out_ref[1, :, h * sub:(h + 1) * sub] = (b_im * q_re - b_re * q_im) / denom

    for h in range(subs):
        for k in range(n_out):
            for r in range(n_in - 1):
                y_copy(k, r, h).wait_send()
        for k in range(n_out - 1):
            d = destination(k)
            for side in range(2):

                @pl.when(d > outer if side == 0 else d < outer)
                def _():
                    z_copy(k, d, h, side).wait_send()

        for step in range(1, n_port):
            g_copy(step, h).wait_send()
    for step in range(1, n_tm):
        p_copy(step).wait_send()
    for step in range(1, n_port):
        m_copy(step).wait_send()


def body(n_tm, n_port, voltages, currents, impedance, freq_index, window_start, pairing):
    ports, local_times = voltages.shape
    width = freq_index.shape[0]
    total = local_times * n_tm
    assert total & (total - 1) == 0 and ports <= 128
    half = math.gcd(local_times // 2, 1024)
    blocks = local_times // (2 * half)
    groups = half // BASE
    lines = width // n_tm
    n_in = 2 if n_tm < 16 else 4
    n_out = n_tm // n_in
    rows = 2 * ports
    subs = 2 if lines % 256 == 0 else 1
    part = (rows, 2 * (lines // subs))
    tall = BASE + groups + blocks
    assert groups % 8 == 0 and blocks % 8 == 0
    sizes = (n_tm, n_in, n_port, ports, half, blocks, lines, groups, width, subs)
    vmem = pl.BlockSpec(memory_space=pltpu.VMEM)
    dma = pltpu.SemaphoreType.DMA
    return pl.pallas_call(
        functools.partial(kernel, sizes),
        out_shape=jax.ShapeDtypeStruct((2, ports, lines), F32),
        in_specs=[
            pl.BlockSpec(memory_space=pl.ANY), pl.BlockSpec(memory_space=pl.ANY),
            vmem, vmem, vmem, pl.BlockSpec(memory_space=pltpu.SMEM),
        ],
        out_specs=vmem,
        scratch_shapes=[
            pltpu.VMEM((tall, width), F32),
            pltpu.VMEM((tall, width), F32),
            pltpu.VMEM((ports, local_times), F32),
            pltpu.VMEM((ports, local_times), F32),
            pltpu.VMEM((blocks * rows, half), jnp.bfloat16),
            pltpu.VMEM((blocks * rows, half), jnp.bfloat16),
            pltpu.VMEM((half, lines), jnp.bfloat16),
            pltpu.VMEM((half, lines), jnp.bfloat16),
            pltpu.VMEM((n_out, n_in - 1, subs) + part, F32),
            pltpu.VMEM((n_out, subs) + part, F32),
            pltpu.VMEM((n_out, n_in - 1, subs) + part, F32),
            pltpu.VMEM((2, n_out, subs) + part, F32),
            pltpu.VMEM((subs, n_port * ports, part[1]), F32),
            pltpu.VMEM((n_tm, 8, 128), F32),
            pltpu.VMEM((n_port, 8, 128), F32),
            pltpu.VMEM((n_port * ports, 128), F32),
            pltpu.VMEM((subs, ports, part[1]), F32),
            pltpu.VMEM((ports, 128), F32),
            dma((2, blocks)),
            dma((n_out, n_in - 1, subs)), dma((n_out, n_in - 1, subs)),
            dma((n_out, subs)), dma((2, n_out, subs)),
            dma((n_port - 1, subs)), dma((n_port - 1, subs)),
            dma((n_tm - 1,)), dma((n_tm - 1,)),
            dma((n_port - 1,)), dma((n_port - 1,)),
        ],
        compiler_params=pltpu.CompilerParams(
            collective_id=0, has_side_effects=True, vmem_limit_bytes=56 * 2**20
        ),
        name="spectra",
    )(voltages, currents, freq_index[None, :], impedance[None, :], window_start[None, :], pairing)


def solution(mesh):
    placed = (P("port", "tm"), P("port", "tm"), P("port"), P(), P("port"), P("port"))
    return jax.shard_map(
        functools.partial(body, mesh.shape["tm"], mesh.shape["port"]),
        mesh=mesh, in_specs=placed, out_specs=P(None, "port", "tm"), check_vma=False,
    )
```

```python
import functools
import math

import jax
import jax.numpy as jnp
from jax import lax
from jax.experimental import pallas as pl
from jax.experimental.pallas import tpu as pltpu
from jax.sharding import PartitionSpec as P

BASE = 32
F32 = jnp.float32


def kernel(
    sizes,
    v_hbm, c_hbm, freq_ref, z_ref, start_ref, pair_ref,
    out_ref,
    cos_ref, sin_ref,
    xv, xc, xe, xo, tab_c, tab_s, away, own, y_recv, z_recv, gath, pbuf, mbuf, mcol, qa, qm,
    load_sem, y_send, y_got, z_send, z_got, g_send, g_got, p_send, p_got, m_send, m_got,
):
    n_tm, n_in, n_port, ports, half, blocks, lines, groups, width, subs = sizes
    sub = lines // subs
    n_out = n_tm // n_in
    rows = 2 * ports
    me = lax.axis_index("tm")
    port = lax.axis_index("port")
    outer, inner = me // n_in, lax.rem(me, n_in)
    span = 2 * half

    def load(block, which):
        source, target = ((v_hbm, xv), (c_hbm, xc))[which]
        return pltpu.make_async_copy(
            source.at[:, pl.ds(pl.multiple_of(block * span, span), span)],
            target.at[:, pl.ds(pl.multiple_of(block * span, span), span)],
            load_sem.at[which, block],
        )

    for block in range(blocks):
        for which in range(2):
            load(block, which).start()

    barrier = pltpu.get_barrier_semaphore()
    for step in range(1, n_tm):
        pl.semaphore_signal(barrier, inc=1, device_id={"tm": lax.rem(me + step, n_tm)})
    for step in range(1, n_port):
        pl.semaphore_signal(barrier, inc=1, device_id={"port": lax.rem(port + step, n_port)})

    flip = (
        lax.broadcasted_iota(jnp.int32, (128, 128), 0)
        + lax.broadcasted_iota(jnp.int32, (128, 128), 1)
        == 127
    ).astype(F32).astype(jnp.bfloat16)
    tiles = half // 128
    lane = lax.broadcasted_iota(jnp.int32, (ports, 128), 1)
    square = lax.broadcasted_iota(jnp.int32, (ports, ports), 0) == lax.broadcasted_iota(
        jnp.int32, (ports, ports), 1
    )

    def column_of(row):
        return jnp.sum(jnp.where(square, row, 0.0), axis=1, keepdims=True)

    zcol = column_of(z_ref[...])
    start_column = column_of(start_ref[...].astype(F32)).astype(jnp.int32)
    starts = jnp.broadcast_to(start_column, (ports, 128)) - me * (blocks * span) - lane

    whole = n_tm * blocks * span
    quarter_bits = (whole // 2).bit_length() - 1
    freq = freq_ref[...]
    count = lax.broadcasted_iota(jnp.int32, (8, 1), 0)
    for at in range(0, BASE + groups + blocks, 8):
        scale = 1.0
        if at < BASE:
            steps = 2 * (count + at) + 1
        elif at < BASE + groups:
            steps = 2 * BASE * (count + (at - BASE))
        else:
            scale = 1.0 / math.sqrt(whole)
            steps = me * (2 * blocks * span) + 4 * half * (count + (at - BASE - groups)) + (2 * half - 1)
        phase = (steps * freq) & (2 * whole - 1)
        quarter = (phase + whole // 4) >> quarter_bits
        x = (phase - (quarter << quarter_bits)).astype(F32) * (math.pi / whole)
        xx = x * x
        s = x * (1.0 + xx * (-1 / 6 + xx * (1 / 120 + xx * (-1 / 5040 + xx * (1 / 362880)))))
        c = 1.0 + xx * (-1 / 2 + xx * (1 / 24 + xx * (-1 / 720 + xx * (1 / 40320))))
        swap = (quarter & 1) == 1
        cosine, sine = jnp.where(swap, s, c), jnp.where(swap, c, s)
        cos_ref[at:at + 8, :] = jnp.where(((quarter + 1) & 2) == 2, -cosine, cosine) * scale
        sin_ref[at:at + 8, :] = jnp.where((quarter & 2) == 2, -sine, sine) * scale

    def fold(block, carry):
        for which in range(2):
            load(block, which).wait()
            ref = (xv, xc)[which]

            def piece(tile):
                at = pl.multiple_of(block * span + tile * 128, 128)
                entries = jnp.where(starts <= at, ref[:, pl.ds(at, 128)], 0.0)
                return entries.astype(jnp.bfloat16)

            at_row = pl.multiple_of(block * rows + which * ports, ports)
            for tile in range(tiles):
                later = piece(tiles + tile).astype(F32)
                earlier = jnp.dot(piece(tiles - 1 - tile), flip, preferred_element_type=F32)
                xe[pl.ds(at_row, ports), tile * 128:(tile + 1) * 128] = (later + earlier).astype(jnp.bfloat16)
                xo[pl.ds(at_row, ports), tile * 128:(tile + 1) * 128] = (later - earlier).astype(jnp.bfloat16)
        return carry

    lax.fori_loop(0, blocks, fold, 0)
    pl.semaphore_wait(barrier, n_tm - 1 + n_port - 1)

    def spectra(owner, store):
        at = pl.ds(pl.multiple_of(owner * lines, lines), lines)
        bc, bs = cos_ref[0:BASE, at], sin_ref[0:BASE, at]
        for g in range(groups):
            tc, ts = cos_ref[BASE + g:BASE + g + 1, at], sin_ref[BASE + g:BASE + g + 1, at]
            tab_c[g * BASE:(g + 1) * BASE, :] = (tc * bc - ts * bs).astype(jnp.bfloat16)
            tab_s[g * BASE:(g + 1) * BASE, :] = (ts * bc + tc * bs).astype(jnp.bfloat16)
        even = jnp.dot(xe[...], tab_c[...], preferred_element_type=F32)
        odd = jnp.dot(xo[...], tab_s[...], preferred_element_type=F32)
        re = jnp.zeros((rows, lines), F32)
        im = jnp.zeros((rows, lines), F32)
        for block in range(blocks):
            k = BASE + groups + block
            pc, ps = cos_ref[k:k + 1, at], sin_ref[k:k + 1, at]
            e, o = even[block * rows:(block + 1) * rows], odd[block * rows:(block + 1) * rows]
            re = re + (pc * e - ps * o)
            im = im - (ps * e + pc * o)
        for h in range(subs):
            store[h, :, 0:sub] = re[:, h * sub:(h + 1) * sub]
            store[h, :, sub:2 * sub] = im[:, h * sub:(h + 1) * sub]

    def destination(k):
        last = n_out - 1
        high = outer // (n_out // 2)
        place = high * outer + (1 - high) * (last - outer)
        longer = (last + place - k) // n_out
        row = longer * k + (1 - longer) * (last - k + place)
        return high * row + (1 - high) * (last - row)

    def y_copy(k, r, h):
        return pltpu.make_async_remote_copy(
            src_ref=away.at[k, r, h], dst_ref=y_recv.at[k, r, h],
            send_sem=y_send.at[k, r, h], recv_sem=y_got.at[k, r, h],
            device_id={"tm": outer * n_in + lax.rem(inner + 1 + r, n_in)},
        )

    def z_copy(k, d, h, side):
        step = 1 - 2 * side
        return pltpu.make_async_remote_copy(
            src_ref=own.at[k, h], dst_ref=z_recv.at[side, d, h],
            send_sem=z_send.at[k, h], recv_sem=z_got.at[side, d, h],
            device_id={"tm": (outer + step) * n_in + inner},
        )

    def add_side(k, d, h, side):
        @pl.when(outer > 0 if side == 0 else outer < n_out - 1)
        def _():
            z_copy(k, d, h, side).wait_recv()
            own[k, h] = own[k, h] + z_recv[side, d, h]

    def collect(k, h):
        for r in range(n_in - 1):
            y_copy(k, r, h).wait_recv()
            own[k, h] = own[k, h] + y_recv[k, r, h]

    def service(k):
        d = destination(k)
        for h in range(subs):
            collect(k, h)

            @pl.when(d > outer)
            def _():
                add_side(k, d, h, 0)
                z_copy(k, d, h, 0).start()

            @pl.when(d < outer)
            def _():
                add_side(k, d, h, 1)
                z_copy(k, d, h, 1).start()

    def stage(k, carry):
        target = destination(k)
        for r in range(n_in - 1):
            spectra(target * n_in + lax.rem(inner + 1 + r, n_in), away.at[k, r])
            for h in range(subs):
                y_copy(k, r, h).start()
        spectra(target * n_in + inner, own.at[k])

        @pl.when(k >= 2)
        def _():
            service(k - 2)

        return carry

    lax.fori_loop(0, n_out, stage, 0)
    service(n_out - 2)

    mine = pl.ds(pl.multiple_of(port * ports, ports), ports)

    def g_copy(step, h):
        return pltpu.make_async_remote_copy(
            src_ref=gath.at[h, mine, :], dst_ref=gath.at[h, mine, :],
            send_sem=g_send.at[step - 1, h], recv_sem=g_got.at[step - 1, h],
            device_id={"port": lax.rem(port + step, n_port)},
        )

    root = 2.0 * jnp.sqrt(zcol)
    power = jnp.zeros((ports, 1), F32)
    for h in range(subs):
        collect(n_out - 1, h)
        add_side(n_out - 1, outer, h, 0)
        add_side(n_out - 1, outer, h, 1)
        volts, amps = own[n_out - 1, h, 0:ports], own[n_out - 1, h, ports:2 * ports]
        a = (volts + zcol * amps) / root
        gath[h, mine, :] = a
        for step in range(1, n_port):
            g_copy(step, h).start()
        power = power + jnp.sum(a * a, axis=1, keepdims=True)

    def p_copy(step):
        return pltpu.make_async_remote_copy(
            src_ref=pbuf.at[0], dst_ref=pbuf.at[step],
            send_sem=p_send.at[step - 1], recv_sem=p_got.at[step - 1],
            device_id={"tm": lax.rem(me + step, n_tm)},
        )

    def m_copy(step):
        return pltpu.make_async_remote_copy(
            src_ref=mbuf.at[port], dst_ref=mbuf.at[port],
            send_sem=m_send.at[step - 1], recv_sem=m_got.at[step - 1],
            device_id={"port": lax.rem(port + step, n_port)},
        )

    diagonal = lane == lax.broadcasted_iota(jnp.int32, (ports, 128), 0)
    packed = jnp.sum(jnp.where(diagonal, power, 0.0), axis=0, keepdims=True)
    pbuf[0] = jnp.broadcast_to(packed, (8, 128))
    for step in range(1, n_tm):
        p_copy(step).start()
    powers = pbuf[0]
    for step in range(1, n_tm):
        p_copy(step).wait_recv()
        powers = powers + pbuf[step]
    mbuf[port] = powers / width + 1e-06
    for step in range(1, n_port):
        m_copy(step).start()
    for h in range(subs):
        for step in range(1, n_port):
            g_copy(step, h).wait_recv()
    for h in range(subs):
        for p in range(ports):
            qa[h, p:p + 1, :] = gath[h, pl.ds(pair_ref[p], 1), :]
        volts, amps = own[n_out - 1, h, 0:ports], own[n_out - 1, h, ports:2 * ports]
        b = (volts - zcol * amps) / root
        b_re, b_im = b[:, 0:sub], b[:, sub:2 * sub]
        q_re, q_im = qa[h, :, 0:sub], qa[h, :, sub:2 * sub]
        out_ref[0, :, h * sub:(h + 1) * sub] = b_re * q_re + b_im * q_im
        out_ref[1, :, h * sub:(h + 1) * sub] = b_im * q_re - b_re * q_im
    for step in range(1, n_port):
        m_copy(step).wait_recv()
    for index in range(n_port):
        spread = jnp.broadcast_to(mbuf[index][0:1, :], (ports, 128))
        column = jnp.sum(jnp.where(diagonal, spread, 0.0), axis=1, keepdims=True)
        mcol[index * ports:(index + 1) * ports, :] = jnp.broadcast_to(column, (ports, 128))
    for p in range(ports):
        qm[p:p + 1, :] = mcol[pl.ds(pair_ref[p], 1), :]
    least = 0.1 * qm[:, 0:1]
    for h in range(subs):
        q_re, q_im = qa[h, :, 0:sub], qa[h, :, sub:2 * sub]
        denom = jnp.maximum(q_re * q_re + q_im * q_im, least)
        for part in range(2):
            at = (part, slice(None), slice(h * sub, (h + 1) * sub))
            out_ref[at] = out_ref[at] / denom

    for h in range(subs):
        for k in range(n_out):
            for r in range(n_in - 1):
                y_copy(k, r, h).wait_send()
        for k in range(n_out - 1):
            d = destination(k)
            for side in range(2):

                @pl.when(d > outer if side == 0 else d < outer)
                def _():
                    z_copy(k, d, h, side).wait_send()

        for step in range(1, n_port):
            g_copy(step, h).wait_send()
    for step in range(1, n_tm):
        p_copy(step).wait_send()
    for step in range(1, n_port):
        m_copy(step).wait_send()


def body(n_tm, n_port, voltages, currents, impedance, freq_index, window_start, pairing):
    ports, local_times = voltages.shape
    width = freq_index.shape[0]
    total = local_times * n_tm
    assert total & (total - 1) == 0 and ports <= 128
    half = math.gcd(local_times // 2, 1024)
    blocks = local_times // (2 * half)
    groups = half // BASE
    lines = width // n_tm
    n_in = 2 if n_tm < 16 else 4
    n_out = n_tm // n_in
    rows = 2 * ports
    subs = 2 if lines % 256 == 0 else 1
    part = (rows, 2 * (lines // subs))
    tall = BASE + groups + blocks
    assert groups % 8 == 0 and blocks % 8 == 0
    sizes = (n_tm, n_in, n_port, ports, half, blocks, lines, groups, width, subs)
    vmem = pl.BlockSpec(memory_space=pltpu.VMEM)
    dma = pltpu.SemaphoreType.DMA
    return pl.pallas_call(
        functools.partial(kernel, sizes),
        out_shape=jax.ShapeDtypeStruct((2, ports, lines), F32),
        in_specs=[
            pl.BlockSpec(memory_space=pl.ANY), pl.BlockSpec(memory_space=pl.ANY),
            vmem, vmem, vmem, pl.BlockSpec(memory_space=pltpu.SMEM),
        ],
        out_specs=vmem,
        scratch_shapes=[
            pltpu.VMEM((tall, width), F32),
            pltpu.VMEM((tall, width), F32),
            pltpu.VMEM((ports, local_times), F32),
            pltpu.VMEM((ports, local_times), F32),
            pltpu.VMEM((blocks * rows, half), jnp.bfloat16),
            pltpu.VMEM((blocks * rows, half), jnp.bfloat16),
            pltpu.VMEM((half, lines), jnp.bfloat16),
            pltpu.VMEM((half, lines), jnp.bfloat16),
            pltpu.VMEM((n_out, n_in - 1, subs) + part, F32),
            pltpu.VMEM((n_out, subs) + part, F32),
            pltpu.VMEM((n_out, n_in - 1, subs) + part, F32),
            pltpu.VMEM((2, n_out, subs) + part, F32),
            pltpu.VMEM((subs, n_port * ports, part[1]), F32),
            pltpu.VMEM((n_tm, 8, 128), F32),
            pltpu.VMEM((n_port, 8, 128), F32),
            pltpu.VMEM((n_port * ports, 128), F32),
            pltpu.VMEM((subs, ports, part[1]), F32),
            pltpu.VMEM((ports, 128), F32),
            dma((2, blocks)),
            dma((n_out, n_in - 1, subs)), dma((n_out, n_in - 1, subs)),
            dma((n_out, subs)), dma((2, n_out, subs)),
            dma((n_port - 1, subs)), dma((n_port - 1, subs)),
            dma((n_tm - 1,)), dma((n_tm - 1,)),
            dma((n_port - 1,)), dma((n_port - 1,)),
        ],
        compiler_params=pltpu.CompilerParams(
            collective_id=0, has_side_effects=True, vmem_limit_bytes=56 * 2**20
        ),
        name="spectra",
    )(voltages, currents, freq_index[None, :], impedance[None, :], window_start[None, :], pairing)


def solution(mesh):
    placed = (P("port", "tm"), P("port", "tm"), P("port"), P(), P("port"), P("port"))
    return jax.shard_map(
        functools.partial(body, mesh.shape["tm"], mesh.shape["port"]),
        mesh=mesh, in_specs=placed, out_specs=P(None, "port", "tm"), check_vma=False,
    )
```

```python
import functools
import math

import jax
import jax.numpy as jnp
from jax import lax
from jax.experimental import pallas as pl
from jax.experimental.pallas import tpu as pltpu
from jax.sharding import PartitionSpec as P

BASE = 32
F32 = jnp.float32


def kernel(
    sizes,
    v_hbm, c_hbm, freq_ref, z_ref, start_ref, row_ref, pair_ref,
    out_ref,
    cos_ref, sin_ref,
    xv, xc, xe, xo, tab_c, tab_s, away, own, y_recv, z_recv, gath, pbuf, mbuf, qa,
    load_sem, y_send, y_got, z_send, z_got, g_send, g_got, p_send, p_got, m_send, m_got,
):
    n_tm, n_in, n_port, ports, half, blocks, lines, groups, width, subs = sizes
    sub = lines // subs
    n_out = n_tm // n_in
    rows = 2 * ports
    me = lax.axis_index("tm")
    port = lax.axis_index("port")
    outer, inner = me // n_in, lax.rem(me, n_in)
    span = 2 * half

    def load(block, which):
        source, target = ((v_hbm, xv), (c_hbm, xc))[which]
        return pltpu.make_async_copy(
            source.at[:, pl.ds(pl.multiple_of(block * span, span), span)],
            target.at[:, pl.ds(pl.multiple_of(block * span, span), span)],
            load_sem.at[which, block],
        )

    for block in range(blocks):
        for which in range(2):
            load(block, which).start()

    barrier = pltpu.get_barrier_semaphore()
    for step in range(1, n_tm):
        pl.semaphore_signal(barrier, inc=1, device_id={"tm": lax.rem(me + step, n_tm)})
    for step in range(1, n_port):
        pl.semaphore_signal(barrier, inc=1, device_id={"port": lax.rem(port + step, n_port)})

    flip = (
        lax.broadcasted_iota(jnp.int32, (128, 128), 0)
        + lax.broadcasted_iota(jnp.int32, (128, 128), 1)
        == 127
    ).astype(F32).astype(jnp.bfloat16)
    tiles = half // 128
    lane = lax.broadcasted_iota(jnp.int32, (ports, 128), 1)
    square = lax.broadcasted_iota(jnp.int32, (ports, ports), 0) == lax.broadcasted_iota(
        jnp.int32, (ports, ports), 1
    )

    def column_of(row):
        return jnp.sum(jnp.where(square, row, 0.0), axis=1, keepdims=True)

    zcol = column_of(z_ref[...])
    start_column = column_of(start_ref[...].astype(F32)).astype(jnp.int32)
    pair_column = column_of(row_ref[...].astype(F32)).astype(jnp.int32)
    starts = jnp.broadcast_to(start_column, (ports, 128)) - me * (blocks * span) - lane

    whole = n_tm * blocks * span
    quarter_bits = (whole // 2).bit_length() - 1
    freq = freq_ref[...]
    count = lax.broadcasted_iota(jnp.int32, (8, 1), 0)
    for at in range(0, BASE + groups + blocks, 8):
        scale = 1.0
        if at < BASE:
            steps = 2 * (count + at) + 1
        elif at < BASE + groups:
            steps = 2 * BASE * (count + (at - BASE))
        else:
            scale = 1.0 / math.sqrt(whole)
            steps = me * (2 * blocks * span) + 4 * half * (count + (at - BASE - groups)) + (2 * half - 1)
        phase = (steps * freq) & (2 * whole - 1)
        quarter = (phase + whole // 4) >> quarter_bits
        x = (phase - (quarter << quarter_bits)).astype(F32) * (math.pi / whole)
        xx = x * x
        s = x * (1.0 + xx * (-1 / 6 + xx * (1 / 120 + xx * (-1 / 5040 + xx * (1 / 362880)))))
        c = 1.0 + xx * (-1 / 2 + xx * (1 / 24 + xx * (-1 / 720 + xx * (1 / 40320))))
        swap = (quarter & 1) == 1
        cosine, sine = jnp.where(swap, s, c), jnp.where(swap, c, s)
        cos_ref[at:at + 8, :] = jnp.where(((quarter + 1) & 2) == 2, -cosine, cosine) * scale
        sin_ref[at:at + 8, :] = jnp.where((quarter & 2) == 2, -sine, sine) * scale

    def fold(block, carry):
        for which in range(2):
            load(block, which).wait()
            ref = (xv, xc)[which]

            def piece(tile):
                at = pl.multiple_of(block * span + tile * 128, 128)
                entries = jnp.where(starts <= at, ref[:, pl.ds(at, 128)], 0.0)
                return entries.astype(jnp.bfloat16)

            at_row = pl.multiple_of(block * rows + which * ports, ports)
            for tile in range(tiles):
                later = piece(tiles + tile).astype(F32)
                earlier = jnp.dot(piece(tiles - 1 - tile), flip, preferred_element_type=F32)
                xe[pl.ds(at_row, ports), tile * 128:(tile + 1) * 128] = (later + earlier).astype(jnp.bfloat16)
                xo[pl.ds(at_row, ports), tile * 128:(tile + 1) * 128] = (later - earlier).astype(jnp.bfloat16)
        return carry

    lax.fori_loop(0, blocks, fold, 0)
    pl.semaphore_wait(barrier, n_tm - 1 + n_port - 1)

    def spectra(owner, store):
        at = pl.ds(pl.multiple_of(owner * lines, lines), lines)
        bc, bs = cos_ref[0:BASE, at], sin_ref[0:BASE, at]
        for g in range(groups):
            tc, ts = cos_ref[BASE + g:BASE + g + 1, at], sin_ref[BASE + g:BASE + g + 1, at]
            tab_c[g * BASE:(g + 1) * BASE, :] = (tc * bc - ts * bs).astype(jnp.bfloat16)
            tab_s[g * BASE:(g + 1) * BASE, :] = (ts * bc + tc * bs).astype(jnp.bfloat16)
        even = jnp.dot(xe[...], tab_c[...], preferred_element_type=F32)
        odd = jnp.dot(xo[...], tab_s[...], preferred_element_type=F32)
        re = jnp.zeros((rows, lines), F32)
        im = jnp.zeros((rows, lines), F32)
        for block in range(blocks):
            k = BASE + groups + block
            pc, ps = cos_ref[k:k + 1, at], sin_ref[k:k + 1, at]
            e, o = even[block * rows:(block + 1) * rows], odd[block * rows:(block + 1) * rows]
            re = re + (pc * e - ps * o)
            im = im - (ps * e + pc * o)
        for h in range(subs):
            store[h, :, 0:sub] = re[:, h * sub:(h + 1) * sub]
            store[h, :, sub:2 * sub] = im[:, h * sub:(h + 1) * sub]

    def destination(k):
        last = n_out - 1
        high = outer // (n_out // 2)
        place = high * outer + (1 - high) * (last - outer)
        longer = (last + place - k) // n_out
        row = longer * k + (1 - longer) * (last - k + place)
        return high * row + (1 - high) * (last - row)

    def y_copy(k, r, h):
        return pltpu.make_async_remote_copy(
            src_ref=away.at[k, r, h], dst_ref=y_recv.at[k, r, h],
            send_sem=y_send.at[k, r, h], recv_sem=y_got.at[k, r, h],
            device_id={"tm": outer * n_in + lax.rem(inner + 1 + r, n_in)},
        )

    def z_copy(k, d, h, side):
        step = 1 - 2 * side
        return pltpu.make_async_remote_copy(
            src_ref=own.at[k, h], dst_ref=z_recv.at[side, d, h],
            send_sem=z_send.at[k, h], recv_sem=z_got.at[side, d, h],
            device_id={"tm": (outer + step) * n_in + inner},
        )

    def add_side(k, d, h, side):
        @pl.when(outer > 0 if side == 0 else outer < n_out - 1)
        def _():
            z_copy(k, d, h, side).wait_recv()
            own[k, h] = own[k, h] + z_recv[side, d, h]

    def collect(k, h):
        for r in range(n_in - 1):
            y_copy(k, r, h).wait_recv()
            own[k, h] = own[k, h] + y_recv[k, r, h]

    def service(k):
        d = destination(k)
        for h in range(subs):
            collect(k, h)

            @pl.when(d > outer)
            def _():
                add_side(k, d, h, 0)
                z_copy(k, d, h, 0).start()

            @pl.when(d < outer)
            def _():
                add_side(k, d, h, 1)
                z_copy(k, d, h, 1).start()

    def stage(k, carry):
        target = destination(k)
        for r in range(n_in - 1):
            spectra(target * n_in + lax.rem(inner + 1 + r, n_in), away.at[k, r])
            for h in range(subs):
                y_copy(k, r, h).start()
        spectra(target * n_in + inner, own.at[k])

        @pl.when(k >= 2)
        def _():
            service(k - 2)

        return carry

    lax.fori_loop(0, n_out, stage, 0)
    service(n_out - 2)

    mine = pl.ds(pl.multiple_of(port * ports, ports), ports)

    def g_copy(step, h):
        return pltpu.make_async_remote_copy(
            src_ref=gath.at[h, mine, :], dst_ref=gath.at[h, mine, :],
            send_sem=g_send.at[step - 1, h], recv_sem=g_got.at[step - 1, h],
            device_id={"port": lax.rem(port + step, n_port)},
        )

    root = 2.0 * jnp.sqrt(zcol)
    power = jnp.zeros((ports, 1), F32)
    for h in range(subs):
        collect(n_out - 1, h)
        add_side(n_out - 1, outer, h, 0)
        add_side(n_out - 1, outer, h, 1)
        volts, amps = own[n_out - 1, h, 0:ports], own[n_out - 1, h, ports:2 * ports]
        a = (volts + zcol * amps) / root
        gath[h, mine, :] = a
        for step in range(1, n_port):
            g_copy(step, h).start()
        power = power + jnp.sum(a * a, axis=1, keepdims=True)

    def p_copy(step):
        return pltpu.make_async_remote_copy(
            src_ref=pbuf.at[0], dst_ref=pbuf.at[step],
            send_sem=p_send.at[step - 1], recv_sem=p_got.at[step - 1],
            device_id={"tm": lax.rem(me + step, n_tm)},
        )

    def m_copy(step):
        return pltpu.make_async_remote_copy(
            src_ref=mbuf.at[port], dst_ref=mbuf.at[port],
            send_sem=m_send.at[step - 1], recv_sem=m_got.at[step - 1],
            device_id={"port": lax.rem(port + step, n_port)},
        )

    diagonal = lane == lax.broadcasted_iota(jnp.int32, (ports, 128), 0)
    packed = jnp.sum(jnp.where(diagonal, power, 0.0), axis=0, keepdims=True)
    pbuf[0] = jnp.broadcast_to(packed, (8, 128))
    for step in range(1, n_tm):
        p_copy(step).start()
    powers = pbuf[0]
    for step in range(1, n_tm):
        p_copy(step).wait_recv()
        powers = powers + pbuf[step]
    mbuf[port] = powers / width + 1e-06
    for step in range(1, n_port):
        m_copy(step).start()
    for h in range(subs):
        for step in range(1, n_port):
            g_copy(step, h).wait_recv()
    for h in range(subs):
        for p in range(ports):
            qa[h, p:p + 1, :] = gath[h, pl.ds(pair_ref[p], 1), :]
        volts, amps = own[n_out - 1, h, 0:ports], own[n_out - 1, h, ports:2 * ports]
        b = (volts - zcol * amps) / root
        b_re, b_im = b[:, 0:sub], b[:, sub:2 * sub]
        q_re, q_im = qa[h, :, 0:sub], qa[h, :, sub:2 * sub]
        out_ref[0, :, h * sub:(h + 1) * sub] = b_re * q_re + b_im * q_im
        out_ref[1, :, h * sub:(h + 1) * sub] = b_im * q_re - b_re * q_im
    for step in range(1, n_port):
        m_copy(step).wait_recv()
    chosen = jnp.zeros((ports, 128), F32)
    for index in range(n_port):
        spread = jnp.broadcast_to(mbuf[index][0:1, :], (ports, 128))
        hit = (lane + index * ports == pair_column) & (lane < ports)
        chosen = chosen + jnp.where(hit, spread, 0.0)
    least = 0.1 * jnp.sum(chosen, axis=1, keepdims=True)
    for h in range(subs):
        q_re, q_im = qa[h, :, 0:sub], qa[h, :, sub:2 * sub]
        denom = jnp.maximum(q_re * q_re + q_im * q_im, least)
        for part in range(2):
            at = (part, slice(None), slice(h * sub, (h + 1) * sub))
            out_ref[at] = out_ref[at] / denom

    for h in range(subs):
        for k in range(n_out):
            for r in range(n_in - 1):
                y_copy(k, r, h).wait_send()
        for k in range(n_out - 1):
            d = destination(k)
            for side in range(2):

                @pl.when(d > outer if side == 0 else d < outer)
                def _():
                    z_copy(k, d, h, side).wait_send()

        for step in range(1, n_port):
            g_copy(step, h).wait_send()
    for step in range(1, n_tm):
        p_copy(step).wait_send()
    for step in range(1, n_port):
        m_copy(step).wait_send()


def body(n_tm, n_port, voltages, currents, impedance, freq_index, window_start, pairing):
    ports, local_times = voltages.shape
    width = freq_index.shape[0]
    total = local_times * n_tm
    assert total & (total - 1) == 0 and ports <= 128
    half = math.gcd(local_times // 2, 1024)
    blocks = local_times // (2 * half)
    groups = half // BASE
    lines = width // n_tm
    n_in = 2 if n_tm < 16 else 4
    n_out = n_tm // n_in
    rows = 2 * ports
    subs = 2 if lines % 256 == 0 else 1
    part = (rows, 2 * (lines // subs))
    tall = BASE + groups + blocks
    assert groups % 8 == 0 and blocks % 8 == 0
    sizes = (n_tm, n_in, n_port, ports, half, blocks, lines, groups, width, subs)
    vmem = pl.BlockSpec(memory_space=pltpu.VMEM)
    dma = pltpu.SemaphoreType.DMA
    return pl.pallas_call(
        functools.partial(kernel, sizes),
        out_shape=jax.ShapeDtypeStruct((2, ports, lines), F32),
        in_specs=[
            pl.BlockSpec(memory_space=pl.ANY), pl.BlockSpec(memory_space=pl.ANY),
            vmem, vmem, vmem, vmem, pl.BlockSpec(memory_space=pltpu.SMEM),
        ],
        out_specs=vmem,
        scratch_shapes=[
            pltpu.VMEM((tall, width), F32),
            pltpu.VMEM((tall, width), F32),
            pltpu.VMEM((ports, local_times), F32),
            pltpu.VMEM((ports, local_times), F32),
            pltpu.VMEM((blocks * rows, half), jnp.bfloat16),
            pltpu.VMEM((blocks * rows, half), jnp.bfloat16),
            pltpu.VMEM((half, lines), jnp.bfloat16),
            pltpu.VMEM((half, lines), jnp.bfloat16),
            pltpu.VMEM((n_out, n_in - 1, subs) + part, F32),
            pltpu.VMEM((n_out, subs) + part, F32),
            pltpu.VMEM((n_out, n_in - 1, subs) + part, F32),
            pltpu.VMEM((2, n_out, subs) + part, F32),
            pltpu.VMEM((subs, n_port * ports, part[1]), F32),
            pltpu.VMEM((n_tm, 8, 128), F32),
            pltpu.VMEM((n_port, 8, 128), F32),
            pltpu.VMEM((subs, ports, part[1]), F32),
            dma((2, blocks)),
            dma((n_out, n_in - 1, subs)), dma((n_out, n_in - 1, subs)),
            dma((n_out, subs)), dma((2, n_out, subs)),
            dma((n_port - 1, subs)), dma((n_port - 1, subs)),
            dma((n_tm - 1,)), dma((n_tm - 1,)),
            dma((n_port - 1,)), dma((n_port - 1,)),
        ],
        compiler_params=pltpu.CompilerParams(
            collective_id=0, has_side_effects=True, vmem_limit_bytes=56 * 2**20
        ),
        name="spectra",
    )(voltages, currents, freq_index[None, :], impedance[None, :], window_start[None, :], pairing[None, :], pairing)


def solution(mesh):
    placed = (P("port", "tm"), P("port", "tm"), P("port"), P(), P("port"), P("port"))
    return jax.shard_map(
        functools.partial(body, mesh.shape["tm"], mesh.shape["port"]),
        mesh=mesh, in_specs=placed, out_specs=P(None, "port", "tm"), check_vma=False,
    )
```
